128 devices in a mesh: seq: 8 (over z, core), exp: 16 (over x, y).
Axes of the slice: x: 4, y: 4, z: 4, core: 2. Of those that a mesh axis runs over, the one named last changes fastest.
Arguments:
- residual: bfloat16 [16384, 8192], P(('seq', 'exp')), may hold values from -6 to 6
- expert_rows: bfloat16 [8, 16, 16, 24, 8192], P('seq', 'exp'), may hold values from -6 to 6
- expert_ids: int32 [16384, 2], P(('seq', 'exp')), may hold values from 0 to 15, as said below
- expert_slots: int32 [16384, 2], P(('seq', 'exp')), may hold values from 0 to 23, as said below
- combine_weights: float32 [16384, 2], P(('seq', 'exp')), may hold values from 0.1 to 0.9
- norm_gain: float32 [8192], replicated, may hold values from 0.1 to 1.9
- in_weight: bfloat16 [8192, 8192], P(None, 'exp'), may hold values from -0.0625 to 0.0625
- conv_weight: float32 [4, 8192], P(None, 'exp'), may hold values from -3 to 3
- conv_bias: float32 [8192], P('exp'), may hold values from -0.5 to 0.5
- bc_weight: bfloat16 [8192, 128], P('exp'), may hold values from -0.00390625 to 0.00390625
- dt_weight: bfloat16 [8192, 128], P('exp'), may hold values from -0.0625 to 0.0625
- dt_bias: float32 [128], P('exp'), may hold values from -2 to 0.5
- decay_log: float32 [128], P('exp'), may hold values from -14 to -3.2
- skip_gain: float32 [128], P('exp'), may hold values from -1 to 3
Outputs:
- scan_output: bfloat16 [16384, 8192], P('seq', 'exp')
The draws below stay inside these ranges and needn't reach their ends.
Inputs may be any that keep to these rules, and one draw needn't show every extreme that they name: `expert_ids`: A token's two ids differ. The tokens of one device name no expert more than 24 times, and in each span one expert is named exactly 24 times by the tokens of every device of the span. `expert_slots`: A token's slot at its k-th expert counts the earlier (token, k) pairs of the same device, in row-major order, that name the same expert.
All inputs are finite; a program needn't handle non-finite values.
Results may differ from the reference program's by a relative error of at most 0.0074.
Values may be sent and summed in bfloat16 or wider, within the bound.
No kernel may reach another device: no remote copies, remote signals or barrier semaphores. Data moves between devices by JAX's collectives and lax.ppermute only.
A program may use at most 320 MiB of HBM per device.

```python
import jax
import jax.numpy as jnp
from jax import lax

D = 8192
TOPK = 2
KCONV = 4
EXPERTS = 16
CH = 8192
HEAD = 64
NSTATE = 64
HEADS = 128
STRETCH = 256
TOK_DEV = 128
CAP = 24
TOKENS = 16384
N_SEQ = 8
N_EXP = 16


def routing_tables(key):
    base_key = jax.random.fold_in(key, 11)
    owners = TOKENS // TOK_DEV
    others = EXPERTS - 1
    remaining = TOPK * TOK_DEV - CAP
    base_load = remaining // others
    extra_count = remaining % others
    pair_count = others // 2
    full_key, owner_key = jax.random.split(base_key)
    full_expert = jax.random.randint(full_key, (owners // N_EXP,), 0, EXPERTS)

    def one_owner(single_key, favored):
        sub_keys = jax.random.split(single_key, 4)
        ordering = jax.random.permutation(sub_keys[0], others)
        chosen = (favored + 1 + ordering) % EXPERTS
        load_sizes = base_load + (jnp.arange(others) < extra_count).astype(jnp.int32)
        shifts = jax.random.randint(sub_keys[1], (pair_count,), 0, base_load // 3 + 1)
        load_sizes = load_sizes.at[2 * jnp.arange(pair_count)].add(shifts)
        load_sizes = load_sizes.at[2 * jnp.arange(pair_count) + 1].add(-shifts)
        counts = jnp.zeros((EXPERTS,), jnp.int32).at[chosen].set(load_sizes).at[favored].set(CAP)
        labels = jnp.repeat(jnp.arange(EXPERTS, dtype=jnp.int32), counts, total_repeat_length=TOPK * TOK_DEV)
        grouped = labels.reshape(TOPK, TOK_DEV).T
        shuffled = grouped[jax.random.permutation(sub_keys[2], TOK_DEV)]
        flipped = jax.random.randint(sub_keys[3], (TOK_DEV,), 0, 2) == 1
        routed = jnp.where(flipped[:, None], shuffled[:, ::-1], shuffled)
        flat_ids = routed.reshape(-1)
        onehot = (flat_ids[:, None] == jnp.arange(EXPERTS, dtype=jnp.int32)[None, :]).astype(jnp.int32)
        before = jnp.cumsum(onehot, axis=0) - onehot
        slot_index = jnp.sum(before * onehot, axis=1).reshape(TOK_DEV, TOPK)
        return (routed, slot_index)
    favored_each = jnp.repeat(full_expert, N_EXP)
    routed, slot_index = jax.vmap(one_owner)(jax.random.split(owner_key, owners), favored_each)
    return (routed.reshape(TOKENS, TOPK).astype(jnp.int32), slot_index.reshape(TOKENS, TOPK).astype(jnp.int32))


def draw_expert_ids(key, part):
    return routing_tables(key)[0]


def draw_expert_slots(key, part):
    return routing_tables(key)[1]


def draw_decay_log(key, part):
    return jax.random.uniform(key, (HEADS,), jnp.float32, -14.0, -3.2)


def draw_skip_gain(key, part):
    offset_key = jax.random.fold_in(jax.random.fold_in(key, 23), 1)
    return jax.random.uniform(offset_key, (HEADS,), jnp.float32, -1.0, 3.0)


def block_levels(own_key, extent, cuts, low, top_value):
    def one(position, shards_of):
        steps = jax.random.uniform(jax.random.fold_in(jax.random.fold_in(own_key, 6), position), (shards_of,), jnp.float32, low / len(cuts), top_value / len(cuts))
        return jnp.repeat(jnp.exp(steps), extent[position] // shards_of).reshape((-1,) + (1,) * (len(extent) - position - 1))

    level = one(*cuts[0])
    for cut in cuts[1:]:
        level = level * one(*cut)
    return level


def normal_values(stream_key, shape, width, bound, pieces=(), held_as=jnp.bfloat16):
    values = width * jax.random.normal(stream_key, shape, jnp.float32)
    if pieces:
        values = values * block_levels(stream_key, shape, pieces, -0.22, 0.18)
    return jnp.clip(values, -bound, bound).astype(held_as)


def setup_inputs(seed: int = 0) -> dict:
    key_list = jax.random.split(jax.random.key(seed), 15)
    residual = normal_values(key_list[0], (TOKENS, D), 1.0, 6.0, ((0, 128),))
    expert_rows = normal_values(key_list[1], (N_SEQ, EXPERTS, N_EXP, CAP, D), 1.0, 6.0, ((0, 8), (1, 16)))
    expert_ids = draw_expert_ids(jax.random.fold_in(key_list[14], 71), 0)
    expert_slots = draw_expert_slots(jax.random.fold_in(key_list[14], 71), 0)
    combine_weights = jnp.clip(0.1 + 0.79999997 * jax.random.uniform(key_list[4], (TOKENS, TOPK), jnp.float32) ** block_levels(key_list[4], (TOKENS, TOPK), ((0, 128),), -0.2, 0.2), 0.1, 0.9)
    norm_gain = jnp.clip(1.0 + 0.18 * jax.random.normal(key_list[5], (D,), jnp.float32), 0.1, 1.9)
    in_weight = normal_values(key_list[6], (D, CH), D ** -0.5, 0.0625, ((1, 16),))
    conv_weight = normal_values(key_list[7], (KCONV, CH), 0.6, 3.0, ((1, 16),), jnp.float32)
    conv_bias = jnp.clip(jax.random.uniform(key_list[8], (CH,), jnp.float32, -0.5, 0.5) * block_levels(key_list[8], (CH,), ((0, 16),), -0.4, 0.0), -0.5, 0.5)
    bc_weight = normal_values(key_list[9], (CH, 2 * NSTATE), (CH * 256) ** -0.5, 0.00390625, ((0, 16),))
    dt_weight = normal_values(key_list[10], (CH, HEADS), CH ** -0.5, 0.0625, ((0, 16),))
    dt_bias = jnp.clip(-2.0 + 2.5 * jax.random.uniform(key_list[11], (HEADS,), jnp.float32) ** block_levels(key_list[11], (HEADS,), ((0, 16),), -0.2, 0.2), -2.0, 0.5)
    decay_log = draw_decay_log(jax.random.fold_in(key_list[14], 71), 0)
    skip_gain = draw_skip_gain(jax.random.fold_in(key_list[14], 71), 0)
    return dict(residual=residual, expert_rows=expert_rows, expert_ids=expert_ids, expert_slots=expert_slots, combine_weights=combine_weights, norm_gain=norm_gain, in_weight=in_weight, conv_weight=conv_weight, conv_bias=conv_bias, bc_weight=bc_weight, dt_weight=dt_weight, dt_bias=dt_bias, decay_log=decay_log, skip_gain=skip_gain)


def block_terms(b_rows, c_rows, steps_dt, decays, values):
    running = jnp.cumsum(decays, axis=0)
    scores = jnp.dot(c_rows, b_rows.T, preferred_element_type=jnp.float32)
    length = running.shape[0]
    causal = (jnp.arange(length)[:, None] >= jnp.arange(length)[None, :])[:, :, None]
    decay_gap = jnp.where(causal, running[:, None, :] - running[None, :, :], 0.0)
    mixing = jnp.where(causal, jnp.exp(decay_gap) * scores[:, :, None] * steps_dt[None, :, :], 0.0).astype(jnp.bfloat16)
    inside = jnp.einsum('tsh,shp->thp', mixing.astype(jnp.float32), values.astype(jnp.float32))
    carried = jnp.exp(running[-1][None, :] - running) * steps_dt
    states = jnp.einsum('sn,shp->hnp', b_rows.astype(jnp.float32), carried[:, :, None] * values.astype(jnp.float32), precision=lax.Precision.HIGHEST)
    return (running, inside, states, jnp.exp(running[-1]))

def reference(residual, expert_rows, expert_ids, expert_slots, combine_weights, norm_gain, in_weight, conv_weight, conv_bias, bc_weight, dt_weight, dt_bias, decay_log, skip_gain):
    owners = N_SEQ * N_EXP

    def combine_owner(inputs):
        owner, resid_rows, owner_ids, owner_slots, owner_weights = inputs
        buffers = expert_rows[owner // N_EXP, :, owner % N_EXP].reshape(EXPERTS * CAP, D)
        picked = buffers[owner_ids * CAP + owner_slots]
        mixture = jnp.zeros((TOK_DEV, D), jnp.float32)
        for column in range(TOPK):
            mixture = mixture + owner_weights[:, column][:, None] * picked[:, column].astype(jnp.float32)
        stream = resid_rows.astype(jnp.float32) + mixture
        factor = lax.rsqrt(lax.optimization_barrier(jnp.mean(stream * stream, axis=1, keepdims=True)) + 1e-06)
        return (stream * factor * norm_gain[None, :]).astype(jnp.bfloat16)
    normed = lax.map(combine_owner, (jnp.arange(owners, dtype=jnp.int32), residual.reshape(owners, TOK_DEV, D), expert_ids.reshape(owners, TOK_DEV, TOPK), expert_slots.reshape(owners, TOK_DEV, TOPK), combine_weights.reshape(owners, TOK_DEV, TOPK))).reshape(TOKENS, D)
    x_in = jnp.dot(normed, in_weight, preferred_element_type=jnp.float32).astype(jnp.bfloat16)
    padded = jnp.concatenate([jnp.zeros((KCONV - 1, CH), jnp.bfloat16), x_in], axis=0)
    filtered = jnp.zeros((TOKENS, CH), jnp.float32) + conv_bias[None, :]
    for tap in range(KCONV):
        filtered = filtered + conv_weight[tap][None, :] * padded[tap:tap + TOKENS].astype(jnp.float32)
    activated = jax.nn.silu(filtered).astype(jnp.bfloat16)
    state_proj = jnp.dot(activated, bc_weight, preferred_element_type=jnp.float32)
    dt_raw = jnp.dot(activated, dt_weight, preferred_element_type=jnp.float32)
    b_all = state_proj[:, :NSTATE].astype(jnp.bfloat16)
    c_all = state_proj[:, NSTATE:].astype(jnp.bfloat16)
    steps_dt = jax.nn.softplus(dt_raw + dt_bias[None, :])
    decays = -jnp.exp(decay_log)[None, :] * steps_dt
    blocks = TOKENS // STRETCH

    def advance(carried_states, inputs):
        b_rows, c_rows, block_dt, block_decays, values = inputs
        running, inside, states, total = block_terms(b_rows, c_rows, block_dt, block_decays, values)
        across = jnp.exp(running)[:, :, None] * jnp.einsum('tn,hnp->thp', c_rows.astype(jnp.float32), carried_states, precision=lax.Precision.HIGHEST)
        output = inside + across + skip_gain[None, :, None] * values.astype(jnp.float32)
        return (total[:, None, None] * carried_states + states, output.astype(jnp.bfloat16))
    final_states, outputs = lax.scan(advance, jnp.zeros((HEADS, NSTATE, HEAD), jnp.float32), (b_all.reshape(blocks, STRETCH, NSTATE), c_all.reshape(blocks, STRETCH, NSTATE), steps_dt.reshape(blocks, STRETCH, HEADS), decays.reshape(blocks, STRETCH, HEADS), activated.reshape(blocks, STRETCH, HEADS, HEAD)))
    return outputs.reshape(TOKENS, CH)
```

```python
import jax
import jax.numpy as jnp
from jax import lax
from jax.experimental import pallas as pl
from jax.experimental.pallas import tpu as pltpu
from jax.sharding import PartitionSpec as P

KCONV = 4
HEAD = 64
NSTATE = 64
STRETCH = 256
PAIR = 2 * HEAD
F32 = jnp.float32
BF16 = jnp.bfloat16
CHUNKS = 2


def mm(a, b):
    return jnp.dot(a, b, preferred_element_type=F32)


def combine_body(hi_ref, lo_ref, rows_ref, residual_ref, gain_ref, out_ref, stream, square):
    step = pl.program_id(0)
    part = rows_ref.shape[1]
    rows = rows_ref[...]
    value = residual_ref[...].astype(F32) + (mm(hi_ref[...], rows) + mm(lo_ref[...], rows))
    stream[:, pl.ds(pl.multiple_of(step * part, part), part)] = value
    total = jnp.sum(value * value, axis=1, keepdims=True)

    @pl.when(step == 0)
    def _():
        square[...] = total

    @pl.when(step > 0)
    def _():
        square[...] = square[...] + total

    @pl.when(step == pl.num_programs(0) - 1)
    def _():
        width = stream.shape[1]
        factor = lax.rsqrt(square[...] * (1.0 / width) + 1e-06)
        for left in range(0, width, part):
            cut = slice(left, left + part)
            out_ref[:, cut] = (stream[:, cut] * factor * gain_ref[:, cut]).astype(BF16)


def combine(hi, lo, rows, residual, gain):
    own, slots = hi.shape
    width = rows.shape[1]
    part = 1024
    return pl.pallas_call(
        combine_body,
        grid=(width // part,),
        in_specs=[
            pl.BlockSpec((own, slots), lambda i: (0, 0)),
            pl.BlockSpec((own, slots), lambda i: (0, 0)),
            pl.BlockSpec((slots, part), lambda i: (0, i)),
            pl.BlockSpec((own, part), lambda i: (0, i)),
            pl.BlockSpec((1, width), lambda i: (0, 0)),
        ],
        out_specs=pl.BlockSpec((own, width), lambda i: (0, 0)),
        out_shape=jax.ShapeDtypeStruct((own, width), BF16),
        scratch_shapes=[pltpu.VMEM((own, width), F32), pltpu.VMEM((own, 1), F32)],
        name="combine",
    )(hi, lo, rows, residual, gain)


def by_pair(first, second, shape):
    lane = lax.broadcasted_iota(jnp.int32, shape, 1)
    return jnp.where(lane < HEAD, jnp.broadcast_to(first, shape), jnp.broadcast_to(second, shape))


def split(value):
    high = value.astype(BF16)
    return high, (value - high.astype(F32)).astype(BF16)


def states_body(values_ref, b_ref, row_ref, dt_ref, col_ref, starts_ref, final_ref, carry):
    step = pl.program_id(0)

    @pl.when(step == 0)
    def _():
        carry[...] = jnp.zeros_like(carry)

    starts_ref[0] = carry[...]
    row = row_ref[...]
    carried = jnp.exp(row[:, STRETCH - 1 :] - row) * dt_ref[...]
    total = jnp.exp(col_ref[STRETCH - 1 :, :])
    b = b_ref[...].astype(F32)
    for pair in range(values_ref.shape[1] // PAIR):
        cut = slice(pair * PAIR, (pair + 1) * PAIR)
        pair_values = values_ref[:, cut]
        sums = []
        for head in (2 * pair, 2 * pair + 1):
            high, low = split(b * carried[head : head + 1, :])
            sums.append(mm(high, pair_values) + mm(low, pair_values))
        fresh = by_pair(sums[0], sums[1], (NSTATE, PAIR))
        keep = by_pair(
            total[:, 2 * pair : 2 * pair + 1], total[:, 2 * pair + 1 : 2 * pair + 2], (1, PAIR)
        )
        carry[:, cut] = keep * carry[:, cut] + fresh

    @pl.when(step == pl.num_programs(0) - 1)
    def _():
        final_ref[...] = carry[...]


def states_of(values, b_t, row, dt_row, col):
    rows, width = values.shape
    blocks = rows // STRETCH
    heads = row.shape[0]
    return pl.pallas_call(
        states_body,
        grid=(blocks,),
        in_specs=[
            pl.BlockSpec((STRETCH, width), lambda i: (i, 0)),
            pl.BlockSpec((NSTATE, STRETCH), lambda i: (0, i)),
            pl.BlockSpec((heads, STRETCH), lambda i: (0, i)),
            pl.BlockSpec((heads, STRETCH), lambda i: (0, i)),
            pl.BlockSpec((STRETCH, heads), lambda i: (i, 0)),
        ],
        out_specs=[
            pl.BlockSpec((1, NSTATE, width), lambda i: (i, 0, 0)),
            pl.BlockSpec((NSTATE, width), lambda i: (0, 0)),
        ],
        out_shape=[
            jax.ShapeDtypeStruct((blocks, NSTATE, width), F32),
            jax.ShapeDtypeStruct((NSTATE, width), F32),
        ],
        scratch_shapes=[pltpu.VMEM((NSTATE, width), F32)],
        name="states",
    )(values, b_t, row, dt_row, col)


def inside_body(values_ref, b_ref, c_ref, row_ref, dt_ref, col_ref, starts_ref, skip_ref, out_ref):
    scores = mm(c_ref[...], b_ref[...])
    square = (STRETCH, STRETCH)
    causal = lax.broadcasted_iota(jnp.int32, square, 0) >= lax.broadcasted_iota(jnp.int32, square, 1)
    scores = jnp.where(causal, scores, 0.0)
    row = row_ref[...]
    col = col_ref[...]
    dt_row = dt_ref[...]
    grown = jnp.exp(col)
    c = c_ref[...]
    for pair in range(values_ref.shape[1] // PAIR):
        cut = slice(pair * PAIR, (pair + 1) * PAIR)
        pair_values = values_ref[:, cut]
        sums = []
        for head in (2 * pair, 2 * pair + 1):
            gap = jnp.minimum(col[:, head : head + 1] - row[head : head + 1, :], 0.0)
            mixing = (jnp.exp(gap) * scores * dt_row[head : head + 1, :]).astype(BF16)
            sums.append(mm(mixing, pair_values))
        inside = by_pair(sums[0], sums[1], (STRETCH, PAIR))
        high, low = split(starts_ref[0, :, cut])
        across = by_pair(
            grown[:, 2 * pair : 2 * pair + 1],
            grown[:, 2 * pair + 1 : 2 * pair + 2],
            (STRETCH, PAIR),
        ) * (mm(c, high) + mm(c, low))
        out_ref[:, cut] = inside + across + skip_ref[:, cut] * pair_values.astype(F32)


def inside_of(values, b_t, c, row, dt_row, col, starts, skip):
    rows, width = values.shape
    heads = row.shape[0]
    return pl.pallas_call(
        inside_body,
        grid=(rows // STRETCH,),
        in_specs=[
            pl.BlockSpec((STRETCH, width), lambda i: (i, 0)),
            pl.BlockSpec((NSTATE, STRETCH), lambda i: (0, i)),
            pl.BlockSpec((STRETCH, NSTATE), lambda i: (i, 0)),
            pl.BlockSpec((heads, STRETCH), lambda i: (0, i)),
            pl.BlockSpec((heads, STRETCH), lambda i: (0, i)),
            pl.BlockSpec((STRETCH, heads), lambda i: (i, 0)),
            pl.BlockSpec((1, NSTATE, width), lambda i: (i, 0, 0)),
            pl.BlockSpec((1, width), lambda i: (0, 0)),
        ],
        out_specs=pl.BlockSpec((STRETCH, width), lambda i: (i, 0)),
        out_shape=jax.ShapeDtypeStruct((rows, width), F32),
        cost_estimate=pl.CostEstimate(
            flops=40 * rows * STRETCH * heads * HEAD,
            transcendentals=rows * STRETCH * heads,
            bytes_accessed=8 * rows * width,
        ),
        name="inside",
    )(values, b_t, c, row, dt_row, col, starts, skip)


def finish_body(partial_ref, c_ref, long_ref, incoming_ref, out_ref):
    grown = jnp.exp(long_ref[...])
    c = c_ref[...]
    for pair in range(partial_ref.shape[1] // PAIR):
        cut = slice(pair * PAIR, (pair + 1) * PAIR)
        high, low = split(incoming_ref[:, cut])
        scale = by_pair(
            grown[:, 2 * pair : 2 * pair + 1],
            grown[:, 2 * pair + 1 : 2 * pair + 2],
            (STRETCH, PAIR),
        )
        out_ref[:, cut] = (partial_ref[:, cut] + scale * (mm(c, high) + mm(c, low))).astype(BF16)


def finish(partial, c, long_col, incoming):
    rows, width = partial.shape
    heads = long_col.shape[1]
    return pl.pallas_call(
        finish_body,
        grid=(rows // STRETCH,),
        in_specs=[
            pl.BlockSpec((STRETCH, width), lambda i: (i, 0)),
            pl.BlockSpec((STRETCH, NSTATE), lambda i: (i, 0)),
            pl.BlockSpec((STRETCH, heads), lambda i: (i, 0)),
            pl.BlockSpec((NSTATE, width), lambda i: (0, 0)),
        ],
        out_specs=pl.BlockSpec((STRETCH, width), lambda i: (i, 0)),
        out_shape=jax.ShapeDtypeStruct((rows, width), BF16),
        name="finish",
    )(partial, c, long_col, incoming)


def shards(
    residual,
    expert_rows,
    expert_ids,
    expert_slots,
    combine_weights,
    norm_gain,
    in_weight,
    conv_weight,
    conv_bias,
    bc_weight,
    dt_weight,
    dt_bias,
    decay_log,
    skip_gain,
):
    own_rows, width = residual.shape
    members = lax.axis_size("exp")
    returned = lax.all_to_all(expert_rows, "exp", split_axis=2, concat_axis=1, tiled=True)
    capacity = returned.shape[3]
    slots = returned.shape[1] * capacity
    buffers = returned.reshape(slots, width)
    index = expert_ids * capacity + expert_slots
    chosen = index[:, :, None] == jnp.arange(slots, dtype=jnp.int32)[None, None, :]
    weights = jnp.sum(jnp.where(chosen, combine_weights[:, :, None], 0.0), axis=1)
    high = lax.reduce_precision(weights, 8, 7)
    normed = combine(
        high.astype(BF16), (weights - high).astype(BF16), buffers, residual, norm_gain[None, :]
    )
    group_rows = own_rows * members
    local_width = in_weight.shape[1]
    piece = own_rows // CHUNKS
    products = []
    for turn in range(CHUNKS):
        gathered = lax.all_gather(
            normed[turn * piece : (turn + 1) * piece], "exp", axis=0, tiled=True
        )
        products.append(mm(gathered, in_weight).astype(BF16).reshape(members, piece, local_width))
    x_in = jnp.stack(products, axis=1).reshape(group_rows, local_width)

    count = lax.axis_size("seq")
    rim_rows = lax.ppermute(
        x_in[group_rows - (KCONV - 1) :], "seq", [(s, s + 1) for s in range(count - 1)]
    )
    padded = jnp.concatenate([rim_rows, x_in], axis=0)
    filtered = jnp.zeros((group_rows, local_width), F32) + conv_bias[None, :]
    for tap in range(KCONV):
        filtered = filtered + conv_weight[tap][None, :] * padded[tap : tap + group_rows].astype(F32)
    activated = jax.nn.silu(filtered).astype(BF16)

    heads = local_width // HEAD
    state_width = bc_weight.shape[1] // members
    projections = jnp.concatenate(
        [
            bc_weight.reshape(local_width, members, state_width),
            dt_weight.reshape(local_width, members, heads),
        ],
        axis=2,
    ).reshape(local_width, members * (state_width + heads))
    parts = lax.dot_general(
        projections, activated, (((0,), (1,)), ((), ())), preferred_element_type=F32
    ).astype(BF16)
    parts = parts.reshape(members, state_width + heads, group_rows)
    parts = lax.all_to_all(parts, "exp", split_axis=0, concat_axis=0, tiled=True)
    sums = jnp.sum(parts.astype(F32), axis=0)
    maps = lax.all_gather(sums[:state_width].astype(BF16), "exp", axis=0, tiled=True)
    b_t = maps[:NSTATE]
    c = maps[NSTATE:].T
    dt_row = jax.nn.softplus(sums[state_width:] + dt_bias[:, None])
    blocks = group_rows // STRETCH
    decays = (-jnp.exp(decay_log)[:, None] * dt_row).reshape(heads, blocks, STRETCH)
    running = jnp.cumsum(decays, axis=2)
    totals = running[:, :, -1]
    before = jnp.cumsum(totals, axis=1) - totals
    row = running.reshape(heads, group_rows)
    col = row.T
    long_col = (running + before[:, :, None]).reshape(heads, group_rows).T
    span = jnp.sum(totals, axis=1)

    starts, final = states_of(activated, b_t, row, dt_row, col)
    extra = jnp.broadcast_to(jnp.repeat(span, HEAD)[None, :], (8, local_width))
    everyone = lax.all_gather(jnp.concatenate([final, extra], axis=0), "seq", axis=0)
    partial = inside_of(
        activated, b_t, c, row, dt_row, col, starts, jnp.repeat(skip_gain, HEAD)[None, :]
    )
    here = lax.axis_index("seq")
    order = jnp.arange(count)
    spans = everyone[:, NSTATE, :]
    between = (order[None, :] > order[:, None]) & (order[None, :] < here)
    gaps = jnp.sum(jnp.where(between[:, :, None], spans[None, :, :], 0.0), axis=1)
    shares = jnp.where((order < here)[:, None], jnp.exp(gaps), 0.0)
    incoming = jnp.sum(shares[:, None, :] * everyone[:, :NSTATE, :], axis=0)
    return finish(partial, c, long_col, incoming)


def solution(mesh):
    placed = (
        P(("seq", "exp"), None),
        P("seq", "exp", None, None, None),
        P(("seq", "exp"), None),
        P(("seq", "exp"), None),
        P(("seq", "exp"), None),
        P(),
        P(None, "exp"),
        P(None, "exp"),
        P("exp"),
        P("exp", None),
        P("exp", None),
        P("exp"),
        P("exp"),
        P("exp"),
    )
    return jax.shard_map(
        shards, mesh=mesh, in_specs=placed, out_specs=P("seq", "exp"), check_vma=False
    )
```
